128 devices in a mesh: grp: 4 (over x), blk: 32 (over z, y, core).
Axes of the slice: x: 4, y: 4, z: 4, core: 2. Of those that a mesh axis runs over, the one named last changes fastest.
Arguments:
- inv_factor: bfloat16 [768, 384, 384], P(('grp', 'blk')), may hold values from -0.3125 to 0.3125
- coupling: bfloat16 [768, 384, 768], P(('grp', 'blk')), may hold values from -0.75 to 0.75
- boundary: bfloat16 [768, 768, 768], P(('grp', 'blk')), may hold values from -6 to 6
- load_int: bfloat16 [768, 384], P(('grp', 'blk')), may hold values from -6 to 6
- load_bnd: bfloat16 [768, 768], P(('grp', 'blk')), may hold values from -6 to 6
- counts: int32 [128], P(('grp', 'blk')), may hold values from 1 to 6, 512 in all
- tile_owner: int32 [768, 36, 1], P(('grp', 'blk')), may hold values from 0 to 127; in each aligned block of 216 rows (0 to 215, 216 to 431, ..., all dimensions but the last counted through in order) at most 2 rows name the same one
- tile_slot: int32 [768, 36], P(('grp', 'blk')), may hold values from 0 to 63
- vec_owner: int32 [768, 6, 1], P(('grp', 'blk')), may hold values from 0 to 127; in each aligned block of 36 rows (0 to 35, 36 to 71, ..., all dimensions but the last counted through in order) at most 2 rows name the same one
- vec_slot: int32 [768, 6], P(('grp', 'blk')), may hold values from 0 to 15
Outputs:
- assembled: float32 [8192, 128, 128], P(('grp', 'blk'))
- loads: float32 [2048, 128], P(('grp', 'blk'))
The draws below stay inside these ranges and needn't reach their ends.
Inputs may be any that keep to these rules, and one draw needn't show every extreme that they name: `tile_owner`: among the 216 rows of one device, no owner is named by more than 2 tiles. `vec_owner`: among the 36 rows of one device, no owner is named by more than 2 load blocks.
All inputs are finite; a program needn't handle non-finite values. No bound on the sum of `counts` on one device may be relied on, other than what follows from the above.
Results may differ from the reference program's by a relative error of at most 0.004.
Values may be sent and summed in bfloat16 or wider, within the bound.
No kernel may reach another device: no remote copies, remote signals or barrier semaphores. Data moves between devices by JAX's collectives and lax.ppermute only.
A program may use at most 128 MiB of HBM per device.

```python
import math
import jax
import jax.numpy as jnp
import numpy as np
from jax import lax

NI = 384
BLOCK_UNKNOWNS = 128
TILES = 6
EMAX = 6
SLOT_DEV = 64
NB = 768
ETILES = 216
LIVE = 4
CAP = 2
VCAP = 2
VSLOT_DEV = 16
ELEMS = 768
INTERFACE_TILES = 8192
LOAD_BLOCK_COUNT = 2048
DEVICES = 128


def with_ends(result, rng, least, top_value):
    dims = result.shape
    spot = [jax.random.randint(jax.random.fold_in(rng, axis), (), 0, dims[axis]) for axis in range(len(dims))]
    result = result.at[tuple(spot)].set(least)
    longest = dims.index(max(dims))
    spot[longest] = (spot[longest] + 1) % dims[longest]
    return result.at[tuple(spot)].set(top_value)


def block_scale(key, dims, split, least, top_value):
    loudness = 1.0
    for axis_at, shards_of in split:
        draws = jax.random.uniform(jax.random.fold_in(jax.random.fold_in(key, 6), axis_at), (shards_of,), jnp.float32, least / len(split), top_value / len(split))
        loudness = loudness * jnp.repeat(jnp.exp(draws), dims[axis_at] // shards_of).reshape((-1,) + (1,) * (len(dims) - 1 - axis_at))
    return loudness


def profile(number_of, total, most, lean):
    loads = [(1 << 20) // math.isqrt(grade ** lean) + 1 for grade in range(2, number_of + 1)]
    spare, given = total - most - (number_of - 1), [1] * (number_of - 1)
    while spare > 0:
        free = [i for i in range(number_of - 1) if given[i] < most]
        pool, remaining = sum([loads[i] for i in free]), spare
        for i in free:
            more = min(most - given[i], max(1, remaining * loads[i] // pool), spare)
            given[i] = given[i] + more
            spare = spare - more
    return np.array([most] + given)


def ragged_sizes(rng, count, total, most, skew):
    if count == 2:
        one = jax.random.randint(rng, (), max(1, total - most), min(most, total - 1) + 1)
        return jnp.stack([one, total - one])
    lengths = jnp.asarray(profile(count, total, most, skew), jnp.int32)
    twos = (count - 1) // 2
    donor, taker = lengths[1:1 + 2 * twos:2], lengths[2:2 + 2 * twos:2]
    margin = jnp.minimum(donor - 1, most - taker)
    passed = jax.random.randint(jax.random.fold_in(rng, 1), (twos,), 0, 1 << 20) % (margin + 1)
    lengths = lengths.at[1:1 + 2 * twos:2].set(donor - passed).at[2:2 + 2 * twos:2].set(taker + passed)
    return lengths[jax.random.permutation(jax.random.fold_in(rng, 2), count)]


def deal_out(stream_key, own, number, rows, amount, top, reach, lean):
    order = jax.random.permutation(stream_key, amount)
    packed, usual = portions_of(amount, rows * top, reach, lean, True), portions_of(amount, rows * top, reach, lean, False)
    places = jnp.arange(amount)

    def named(lengths, rotation):
        used = int((lengths > 0).sum())
        fixed = max(1, used // 4)
        shifted = fixed + (places - fixed + rotation * (used - fixed)) % max(1, amount - fixed)
        return jnp.zeros((amount,), jnp.int32).at[order[jnp.where(places < fixed, places, shifted)]].set(jnp.asarray(lengths, jnp.int32))

    lengths = jnp.where(number % 4 == 0, named(packed, number // 4), named(usual, number - number // 4 - 1))
    mixed = jax.random.permutation(jax.random.fold_in(own, 3), amount)
    donor, taker = mixed[0:amount // 2 * 2:2], mixed[1:amount // 2 * 2:2]
    margin = jnp.minimum(lengths[donor] - 1, reach - lengths[taker]) // 2
    margin = jnp.where((donor == order[0]) | (taker == order[0]) | (lengths[taker] == 0), 0, jnp.maximum(margin, 0))
    shifted = jax.random.randint(jax.random.fold_in(own, 4), (amount // 2,), 0, 1 << 20) % (margin + 1)
    lengths = lengths.at[donor].add(-shifted).at[taker].add(shifted)
    labels = jnp.searchsorted(jnp.cumsum(lengths), jnp.arange(rows * top), side="right").astype(jnp.int32)
    listing = labels.reshape(top, rows).T
    listing = listing[jax.random.permutation(jax.random.fold_in(own, 1), rows)]
    rotation = jax.random.randint(jax.random.fold_in(own, 2), (rows, 1), 0, top)
    return jnp.take_along_axis(listing, (jnp.arange(top)[None, :] + rotation) % top, axis=1)


def portions_of(number_of, total, most, slope, full):
    loads = [(1 << 20) // math.isqrt(standing ** slope) + 1 for standing in range(1, number_of + 1)]
    largest = most if full else min(most, max(-(-total // number_of), total * loads[0] // sum(loads)))
    least = 1 if total - largest >= number_of - 1 else 0
    holding, rest = [largest] + [least] * (number_of - 1), total - largest - least * (number_of - 1)
    while rest > 0:
        candidates = [i for i in range(1, number_of) if holding[i] < largest] or [i for i in range(1, number_of) if holding[i] < most]
        mass, remaining = sum([loads[i] for i in candidates]), rest
        for i in candidates:
            addition = min(most - holding[i], max(1, remaining * loads[i] // mass), rest)
            holding[i] = holding[i] + addition
            rest = rest - addition
    return np.array(holding)


def gaussian(stream_key, shape, scale, limit, split=(), held_as=jnp.bfloat16):
    level = block_scale(stream_key, shape, split, -0.22, 0.18) if split else 1.0
    result = jax.random.normal(stream_key, shape, jnp.float32) * scale * level
    return jnp.minimum(jnp.maximum(result, -limit), limit).astype(held_as)


def setup_inputs(seed: int = 0) -> dict:
    key_of = jax.random.split(jax.random.key(seed), 11)
    inv_factor = gaussian(key_of[0], (ELEMS, NI, NI), NI ** -0.5, 0.3125, ((0, 128),))
    coupling = gaussian(key_of[1], (ELEMS, NI, NB), 64 ** -0.5, 0.75, ((0, 128),))
    boundary = gaussian(key_of[2], (ELEMS, NB, NB), 1.0, 6.0, ((0, 128),))
    load_int = gaussian(key_of[3], (ELEMS, NI), 1.0, 6.0, ((0, 128),))
    load_bnd = gaussian(key_of[4], (ELEMS, NB), 1.0, 6.0, ((0, 128),))
    counts = ragged_sizes(key_of[5], DEVICES, LIVE * DEVICES, EMAX, 2).astype(jnp.int32)
    tile_owner_keys = jax.random.split(jax.random.fold_in(key_of[6], 1), ELEMS * (TILES * TILES) // ETILES)
    tile_owner_turns = jax.random.permutation(jax.random.fold_in(key_of[6], 3), ELEMS * (TILES * TILES) // ETILES)
    tile_owner = jax.vmap(lambda own, number: deal_out(jax.random.fold_in(key_of[6], 2), own, number, ETILES, DEVICES, 1, CAP, 2))(tile_owner_keys, tile_owner_turns).reshape((ELEMS, TILES * TILES, 1))
    tile_slot = with_ends(jax.random.randint(key_of[7], (ELEMS, TILES * TILES), 0, SLOT_DEV), jax.random.fold_in(key_of[7], 1), 0, SLOT_DEV - 1).astype(jnp.int32)
    vec_owner_keys = jax.random.split(jax.random.fold_in(key_of[8], 1), ELEMS * TILES // (EMAX * TILES))
    vec_owner_turns = jax.random.permutation(jax.random.fold_in(key_of[8], 3), ELEMS * TILES // (EMAX * TILES))
    vec_owner = jax.vmap(lambda own, number: deal_out(jax.random.fold_in(key_of[8], 2), own, number, EMAX * TILES, DEVICES, 1, VCAP, 2))(vec_owner_keys, vec_owner_turns).reshape((ELEMS, TILES, 1))
    vec_slot = with_ends(jax.random.randint(key_of[9], (ELEMS, TILES), 0, VSLOT_DEV), jax.random.fold_in(key_of[9], 1), 0, VSLOT_DEV - 1).astype(jnp.int32)
    return {"inv_factor": inv_factor, "coupling": coupling, "boundary": boundary, "load_int": load_int, "load_bnd": load_bnd, "counts": counts, "tile_owner": tile_owner, "tile_slot": tile_slot, "vec_owner": vec_owner, "vec_slot": vec_slot}


def mult(a, b):
    return jnp.dot(a.astype(jnp.float32), b.astype(jnp.float32), precision=lax.Precision.HIGHEST)


def reference(inv_factor, coupling, boundary, load_int, load_bnd, counts, tile_owner, tile_slot, vec_owner, vec_slot):
    nelem = inv_factor.shape[0]
    nb = boundary.shape[1]
    tiles = nb // BLOCK_UNKNOWNS
    targets = (tile_owner[:, :, 0] * SLOT_DEV + tile_slot).astype(jnp.int32)
    vtargets = (vec_owner[:, :, 0] * VSLOT_DEV + vec_slot).astype(jnp.int32)

    def step(index, carry):
        stiffness_matrices, load_vectors = carry
        elem = jnp.asarray(index).astype(jnp.int32)
        owner_dev = (elem // EMAX).astype(jnp.int32)
        alive = ((elem % EMAX) < lax.dynamic_index_in_dim(counts, owner_dev, 0, keepdims=False)).astype(jnp.float32)
        factor = lax.dynamic_index_in_dim(inv_factor, elem, 0, keepdims=False)
        couple = lax.dynamic_index_in_dim(coupling, elem, 0, keepdims=False)
        bound = lax.dynamic_index_in_dim(boundary, elem, 0, keepdims=False)
        inner = lax.dynamic_index_in_dim(load_int, elem, 0, keepdims=False)
        outer = lax.dynamic_index_in_dim(load_bnd, elem, 0, keepdims=False)
        coupled = mult(factor, couple).astype(jnp.bfloat16)
        schur = (bound.astype(jnp.float32) - mult(coupled.T, coupled)).astype(jnp.bfloat16)
        pulled = mult(factor, inner).astype(jnp.bfloat16)
        condensed = (outer.astype(jnp.float32) - mult(pulled, coupled)).astype(jnp.bfloat16)
        pieces = schur.astype(jnp.float32).reshape(tiles, BLOCK_UNKNOWNS, tiles, BLOCK_UNKNOWNS).transpose(0, 2, 1, 3).reshape(tiles * tiles, BLOCK_UNKNOWNS * BLOCK_UNKNOWNS)
        blocks = condensed.astype(jnp.float32).reshape(tiles, BLOCK_UNKNOWNS)
        rows = lax.dynamic_index_in_dim(targets, elem, 0, keepdims=False)
        vrows = lax.dynamic_index_in_dim(vtargets, elem, 0, keepdims=False)
        stiffness_matrices = stiffness_matrices.at[rows].add(pieces * alive)
        load_vectors = load_vectors.at[vrows].add(blocks * alive)
        return stiffness_matrices, load_vectors

    start_offset = (jnp.zeros((INTERFACE_TILES, BLOCK_UNKNOWNS * BLOCK_UNKNOWNS), jnp.float32), jnp.zeros((LOAD_BLOCK_COUNT, BLOCK_UNKNOWNS), jnp.float32))
    stiffness_matrices, load_vectors = lax.fori_loop(0, nelem, step, start_offset)
    return stiffness_matrices.reshape(INTERFACE_TILES, BLOCK_UNKNOWNS, BLOCK_UNKNOWNS), load_vectors
```

```python
import jax
import jax.numpy as jnp
from jax import lax
from jax.experimental import pallas as pl
from jax.experimental.pallas import tpu as pltpu
from jax.sharding import PartitionSpec as P

TILE = 128
SLOT_DEV = 64
VSLOT_DEV = 16
CAP = 2
HEAD = 8
AXES = ("grp", "blk")
MIB = 1 << 20


def spread(value):
    return jnp.full((1, TILE), value, jnp.int32).astype(jnp.float32)


def row_of(ref, k):
    rows = ref[...].astype(jnp.float32)
    at = lax.broadcasted_iota(jnp.int32, rows.shape, 0) == k
    return jnp.sum(jnp.where(at, rows, 0.0), axis=0, keepdims=True)


def pack_kernel(
    counts,
    owner,
    slot,
    vowner,
    vslot,
    factor_hbm,
    couple_hbm,
    bound_hbm,
    inner,
    outer,
    send,
    factor,
    couple,
    bound,
    pieces,
    left,
    head,
    head16,
    used,
    vused,
    target,
    vtarget,
    in_sem,
    out_sem,
    head_sem,
):
    emax, ni, nb = couple.shape
    tiles = nb // TILE
    per = tiles * tiles
    peers = used.shape[0]
    live = counts[0]

    def loads(k):
        return (
            pltpu.make_async_copy(factor_hbm.at[k], factor.at[k], in_sem.at[0, k]),
            pltpu.make_async_copy(couple_hbm.at[k], couple.at[k], in_sem.at[1, k]),
            pltpu.make_async_copy(bound_hbm.at[k], bound.at[k], in_sem.at[2, k]),
        )

    @pl.loop(0, live)
    def _(k):
        for copy in loads(k):
            copy.start()

    row = lax.broadcasted_iota(jnp.int32, (HEAD, TILE), 0)
    blank = jnp.where((row >= CAP) & (row < 3 * CAP), -1.0, 0.0).astype(jnp.float32)

    @pl.loop(0, peers)
    def _(p):
        used[p] = 0
        vused[p] = 0
        head[pl.ds(pl.multiple_of(p * HEAD, HEAD), HEAD), :] = blank

    @pl.loop(0, live)
    def _(k):
        @pl.loop(0, per)
        def _(t):
            p = owner[k, 0, t]
            r = used[p]
            used[p] = r + 1
            target[k * per + t] = p * CAP + r
            head[pl.ds(p * HEAD + CAP + r, 1), :] = spread(slot[k, t])

        @pl.loop(0, tiles)
        def _(t):
            p = vowner[k, 0, t]
            r = vused[p]
            vused[p] = r + 1
            vtarget[k * tiles + t] = p * HEAD + r
            head[pl.ds(p * HEAD + 2 * CAP + r, 1), :] = spread(vslot[k, t])

    @pl.loop(0, live)
    def _(k):
        for copy in loads(k):
            copy.wait()
        coupled = lax.dot_general(
            couple[k], factor[k], (((0,), (1,)), ((), ())), preferred_element_type=jnp.float32
        ).astype(jnp.bfloat16)
        inner_rows = jnp.broadcast_to(row_of(inner, k), (16, ni)).astype(jnp.bfloat16)
        pulled = lax.dot_general(
            inner_rows, factor[k], (((1,), (1,)), ((), ())), preferred_element_type=jnp.float32
        ).astype(jnp.bfloat16)
        left[pl.ds(0, nb), :] = coupled
        left[pl.ds(nb, 16), :] = pulled
        for a in range(tiles):
            last = a == tiles - 1
            lhs = left[pl.ds(a * TILE, TILE + (16 if last else 0)), :]
            product = lax.dot_general(
                lhs, left[pl.ds(0, nb), :], (((1,), (1,)), ((), ())), preferred_element_type=jnp.float32
            )
            schur = bound[k, pl.ds(a * TILE, TILE), :].astype(jnp.float32) - product[:TILE]
            for b in range(tiles):
                pieces[k, a * tiles + b] = schur[:, b * TILE : (b + 1) * TILE].astype(jnp.bfloat16)
                t = k * per + a * tiles + b
                to = target[t]
                peer = lax.shift_right_logical(to, 1)
                start = pl.multiple_of(HEAD + (to & 1) * TILE, HEAD)
                pltpu.make_async_copy(
                    pieces.at[k, a * tiles + b], send.at[peer, pl.ds(start, TILE), :], out_sem.at[k]
                ).start()
            if last:
                condensed = row_of(outer, k) - product[TILE : TILE + 1]
                for b in range(tiles):
                    head[pl.ds(vtarget[k * tiles + b], 1), :] = condensed[:, b * TILE : (b + 1) * TILE]

    head16[...] = head[...].reshape(peers, HEAD, TILE).astype(jnp.bfloat16)
    head_copy = pltpu.make_async_copy(head16, send.at[:, pl.ds(0, HEAD), :], head_sem)
    head_copy.start()

    @pl.loop(0, live)
    def _(k):
        pltpu.make_async_copy(pieces.at[k], pieces.at[k], out_sem.at[k]).wait()

    head_copy.wait()


def packed(peers, inv_factor, coupling, boundary, load_int, load_bnd, counts, owner, slot, vowner, vslot):
    emax, ni, nb = coupling.shape
    tiles = nb // TILE
    per = tiles * tiles
    smem = pl.BlockSpec(memory_space=pltpu.SMEM)
    hbm = pl.BlockSpec(memory_space=pltpu.HBM)
    vmem = pl.BlockSpec(memory_space=pltpu.VMEM)
    return pl.pallas_call(
        pack_kernel,
        out_shape=jax.ShapeDtypeStruct((peers, HEAD + CAP * TILE, TILE), jnp.bfloat16),
        in_specs=[smem] * 5 + [hbm] * 3 + [vmem] * 2,
        out_specs=hbm,
        scratch_shapes=[
            pltpu.VMEM((emax, ni, ni), jnp.bfloat16),
            pltpu.VMEM((emax, ni, nb), jnp.bfloat16),
            pltpu.VMEM((emax, nb, nb), jnp.bfloat16),
            pltpu.VMEM((emax, per, TILE, TILE), jnp.bfloat16),
            pltpu.VMEM((nb + 16, ni), jnp.bfloat16),
            pltpu.VMEM((peers * HEAD, TILE), jnp.float32),
            pltpu.VMEM((peers, HEAD, TILE), jnp.bfloat16),
            pltpu.SMEM((peers,), jnp.int32),
            pltpu.SMEM((peers,), jnp.int32),
            pltpu.SMEM((emax * per,), jnp.int32),
            pltpu.SMEM((emax * tiles,), jnp.int32),
            pltpu.SemaphoreType.DMA((3, emax)),
            pltpu.SemaphoreType.DMA((emax,)),
            pltpu.SemaphoreType.DMA,
        ],
        compiler_params=pltpu.CompilerParams(vmem_limit_bytes=48 * MIB),
        name="condense_pack",
    )(
        counts,
        owner,
        slot,
        vowner,
        vslot,
        inv_factor,
        coupling,
        boundary,
        load_int,
        load_bnd,
    )


def sum_kernel(got, assembled, loads, head, parts, ids_vec, ids, head_sem, part_sem, ids_sem):
    peers = head.shape[0]
    chunks, width = parts.shape[:2]
    head_copy = pltpu.make_async_copy(got.at[:, pl.ds(0, HEAD), :], head, head_sem)
    head_copy.start()
    for c in range(chunks):
        pltpu.make_async_copy(
            got.at[pl.ds(c * width, width), pl.ds(HEAD, CAP * TILE), :], parts.at[c], part_sem.at[c]
        ).start()

    zero = jnp.zeros((TILE, TILE), jnp.float32)

    @pl.loop(0, SLOT_DEV)
    def _(s):
        assembled[s] = zero

    head_copy.wait()
    rows = head[...].astype(jnp.float32)
    diagonal = lax.broadcasted_iota(jnp.int32, (peers, TILE), 0) == lax.broadcasted_iota(
        jnp.int32, (peers, TILE), 1
    )
    lane = lax.broadcasted_iota(jnp.int32, (peers, TILE), 1).astype(jnp.float32)
    total = jnp.zeros((TILE, TILE), jnp.float32)
    for r in range(CAP):
        named = jnp.where(diagonal, rows[:, CAP + r, :], 0.0)
        ids_vec[pl.ds(r, 1), :] = jnp.sum(named, axis=0, keepdims=True).astype(jnp.int32)
        select = (rows[:, 2 * CAP + r, :] == lane).astype(jnp.bfloat16)
        total += lax.dot_general(
            select,
            rows[:, r, :].astype(jnp.bfloat16),
            (((0,), (0,)), ((), ())),
            preferred_element_type=jnp.float32,
        )
    ids_copy = pltpu.make_async_copy(ids_vec, ids, ids_sem)
    ids_copy.start()
    loads[...] = total[:VSLOT_DEV]
    ids_copy.wait()

    for c in range(chunks):
        pltpu.make_async_copy(
            got.at[pl.ds(c * width, width), pl.ds(HEAD, CAP * TILE), :], parts.at[c], part_sem.at[c]
        ).wait()

        @pl.loop(0, width)
        def _(w):
            for r in range(CAP):
                s = ids[r, c * width + w]

                @pl.when(s >= 0)
                def _():
                    assembled[s] += parts[c, w, pl.ds(r * TILE, TILE), :].astype(jnp.float32)


def summed(got):
    peers = got.shape[0]
    chunks = 8
    hbm = pl.BlockSpec(memory_space=pltpu.HBM)
    vmem = pl.BlockSpec(memory_space=pltpu.VMEM)
    return pl.pallas_call(
        sum_kernel,
        out_shape=(
            jax.ShapeDtypeStruct((SLOT_DEV, TILE, TILE), jnp.float32),
            jax.ShapeDtypeStruct((VSLOT_DEV, TILE), jnp.float32),
        ),
        in_specs=[hbm],
        out_specs=(vmem, vmem),
        scratch_shapes=[
            pltpu.VMEM((peers, HEAD, TILE), jnp.bfloat16),
            pltpu.VMEM((chunks, peers // chunks, CAP * TILE, TILE), jnp.bfloat16),
            pltpu.VMEM((8, TILE), jnp.int32),
            pltpu.SMEM((8, TILE), jnp.int32),
            pltpu.SemaphoreType.DMA,
            pltpu.SemaphoreType.DMA((chunks,)),
            pltpu.SemaphoreType.DMA,
        ],
        compiler_params=pltpu.CompilerParams(vmem_limit_bytes=48 * MIB),
        name="sum_tiles",
    )(got)


def shards(
    inv_factor, coupling, boundary, load_int, load_bnd, counts, tile_owner, tile_slot, vec_owner, vec_slot
):
    peers = lax.axis_size("grp") * lax.axis_size("blk")
    send = packed(
        peers,
        inv_factor,
        coupling,
        boundary,
        load_int,
        load_bnd,
        counts,
        jnp.swapaxes(tile_owner, 1, 2),
        tile_slot,
        jnp.swapaxes(vec_owner, 1, 2),
        vec_slot,
    )
    got = lax.all_to_all(send, AXES, split_axis=0, concat_axis=0, tiled=True)
    return summed(got)


def solution(mesh):
    in_specs = (
        P(AXES, None, None),
        P(AXES, None, None),
        P(AXES, None, None),
        P(AXES, None),
        P(AXES, None),
        P(AXES),
        P(AXES, None, None),
        P(AXES, None),
        P(AXES, None, None),
        P(AXES, None),
    )
    out_specs = (P(AXES, None, None), P(AXES, None))
    return jax.shard_map(shards, mesh=mesh, in_specs=in_specs, out_specs=out_specs, check_vma=False)
```

```python
import jax
import jax.numpy as jnp
from jax import lax
from jax.experimental import pallas as pl
from jax.experimental.pallas import tpu as pltpu
from jax.sharding import PartitionSpec as P

TILE = 128
SLOT_DEV = 64
VSLOT_DEV = 16
CAP = 2
HEAD = 8
WIDE = 256
AXES = ("grp", "blk")
MIB = 1 << 20


def spread(value):
    return jnp.full((1, TILE), value, jnp.int32).astype(jnp.float32)


def row_of(ref, k):
    rows = ref[...].astype(jnp.float32)
    at = lax.broadcasted_iota(jnp.int32, rows.shape, 0) == k
    return jnp.sum(jnp.where(at, rows, 0.0), axis=0, keepdims=True)


def pack_kernel(
    counts,
    owner_hbm,
    slot_hbm,
    vowner_hbm,
    vslot_hbm,
    factor_hbm,
    couple_hbm,
    bound_hbm,
    inner_hbm,
    outer_hbm,
    send,
    owner,
    slot,
    vowner,
    vslot,
    inner,
    outer,
    factor,
    couple,
    bound,
    left,
    head,
    used,
    vused,
    target,
    vtarget,
    table_sem,
    in_sem,
):
    emax, ni, nb = couple.shape
    tiles = nb // TILE
    per = tiles * tiles
    peers = used.shape[0]
    tables = [
        pltpu.make_async_copy(source, held, table_sem.at[i])
        for i, (source, held) in enumerate(
            (
                (owner_hbm, owner),
                (slot_hbm, slot),
                (vowner_hbm, vowner),
                (vslot_hbm, vslot),
                (inner_hbm, inner),
                (outer_hbm, outer),
            )
        )
    ]
    for copy in tables:
        copy.start()
    live = counts[0]

    def loads(k):
        return (
            pltpu.make_async_copy(factor_hbm.at[k], factor.at[k], in_sem.at[0, k]),
            pltpu.make_async_copy(couple_hbm.at[k], couple.at[k], in_sem.at[1, k]),
            pltpu.make_async_copy(bound_hbm.at[k], bound.at[k], in_sem.at[2, k]),
        )

    @pl.loop(0, live)
    def _(k):
        for copy in loads(k):
            copy.start()

    row = lax.broadcasted_iota(jnp.int32, (HEAD, TILE), 0)
    blank = jnp.where((row >= CAP) & (row < 3 * CAP), -1.0, 0.0).astype(jnp.float32)

    @pl.loop(0, peers)
    def _(p):
        used[p] = 0
        vused[p] = 0
        head[pl.ds(pl.multiple_of(p * HEAD, HEAD), HEAD), :] = blank

    for copy in tables:
        copy.wait()

    @pl.loop(0, live)
    def _(k):
        @pl.loop(0, per)
        def _(t):
            p = owner[k, 0, t]
            r = used[p]
            used[p] = r + 1
            target[k * per + t] = p * CAP + r
            head[pl.ds(p * HEAD + CAP + r, 1), :] = spread(slot[k, t])

        @pl.loop(0, tiles)
        def _(t):
            p = vowner[k, 0, t]
            r = vused[p]
            vused[p] = r + 1
            vtarget[k * tiles + t] = p * HEAD + r
            head[pl.ds(p * HEAD + 2 * CAP + r, 1), :] = spread(vslot[k, t])

    @pl.loop(0, live)
    def _(k):
        for copy in loads(k):
            copy.wait()
        coupled = lax.dot_general(
            couple[k], factor[k], (((0,), (1,)), ((), ())), preferred_element_type=jnp.float32
        ).astype(jnp.bfloat16)
        inner_rows = jnp.broadcast_to(row_of(inner, k), (16, ni)).astype(jnp.bfloat16)
        pulled = lax.dot_general(
            inner_rows, factor[k], (((1,), (1,)), ((), ())), preferred_element_type=jnp.float32
        ).astype(jnp.bfloat16)
        outer_rows = row_of(outer, k)
        left[pl.ds(0, nb), :] = coupled
        left[pl.ds(nb, 16), :] = pulled
        for n in range(nb // WIDE):
            product = lax.dot_general(
                left[...],
                left[pl.ds(n * WIDE, WIDE), :],
                (((1,), (1,)), ((), ())),
                preferred_element_type=jnp.float32,
            )
            for a in range(tiles):
                rows = pl.ds(a * TILE, TILE)
                schur = bound[k, rows, pl.ds(n * WIDE, WIDE)].astype(jnp.float32) - product[a * TILE : (a + 1) * TILE]
                for b in range(WIDE // TILE):
                    to = target[k * per + a * tiles + n * (WIDE // TILE) + b]
                    peer = lax.shift_right_logical(to, 1)
                    start = pl.multiple_of(HEAD + (to & 1) * TILE, HEAD)
                    send[peer, pl.ds(start, TILE), :] = schur[:, b * TILE : (b + 1) * TILE].astype(jnp.bfloat16)
            condensed = outer_rows[:, n * WIDE : (n + 1) * WIDE] - product[nb : nb + 1]
            for b in range(WIDE // TILE):
                at = vtarget[k * tiles + n * (WIDE // TILE) + b]
                head[pl.ds(at, 1), :] = condensed[:, b * TILE : (b + 1) * TILE]

    send[:, pl.ds(0, HEAD), :] = head[...].reshape(peers, HEAD, TILE).astype(jnp.bfloat16)


def packed(peers, inv_factor, coupling, boundary, load_int, load_bnd, counts, owner, slot, vowner, vslot):
    emax, ni, nb = coupling.shape
    tiles = nb // TILE
    per = tiles * tiles
    hbm = pl.BlockSpec(memory_space=pltpu.HBM)
    operands = (owner, slot, vowner, vslot, inv_factor, coupling, boundary, load_int, load_bnd)
    return pl.pallas_call(
        pack_kernel,
        out_shape=pltpu.VMEM((peers, HEAD + CAP * TILE, TILE), jnp.bfloat16),
        in_specs=[pl.BlockSpec(memory_space=pltpu.SMEM)] + [hbm] * len(operands),
        out_specs=pl.BlockSpec(memory_space=pltpu.VMEM),
        scratch_shapes=[
            pltpu.SMEM((emax, 1, per), jnp.int32),
            pltpu.SMEM((emax, per), jnp.int32),
            pltpu.SMEM((emax, 1, tiles), jnp.int32),
            pltpu.SMEM((emax, tiles), jnp.int32),
            pltpu.VMEM((emax, ni), jnp.bfloat16),
            pltpu.VMEM((emax, nb), jnp.bfloat16),
            pltpu.VMEM((emax, ni, ni), jnp.bfloat16),
            pltpu.VMEM((emax, ni, nb), jnp.bfloat16),
            pltpu.VMEM((emax, nb, nb), jnp.bfloat16),
            pltpu.VMEM((nb + 16, ni), jnp.bfloat16),
            pltpu.VMEM((peers * HEAD, TILE), jnp.float32),
            pltpu.SMEM((peers,), jnp.int32),
            pltpu.SMEM((peers,), jnp.int32),
            pltpu.SMEM((emax * per,), jnp.int32),
            pltpu.SMEM((emax * tiles,), jnp.int32),
            pltpu.SemaphoreType.DMA((6,)),
            pltpu.SemaphoreType.DMA((3, emax)),
        ],
        compiler_params=pltpu.CompilerParams(vmem_limit_bytes=48 * MIB),
        name="condense_pack",
    )(counts, *(pltpu.with_memory_space_constraint(x, pltpu.HBM) for x in operands))


def sum_kernel(got, assembled, loads, head, parts, ids_vec, ids, head_sem, part_sem, ids_sem):
    peers = head.shape[0]
    chunks, width = parts.shape[:2]
    head_copy = pltpu.make_async_copy(got.at[:, pl.ds(0, HEAD), :], head, head_sem)
    head_copy.start()
    for c in range(chunks):
        pltpu.make_async_copy(
            got.at[pl.ds(c * width, width), pl.ds(HEAD, CAP * TILE), :], parts.at[c], part_sem.at[c]
        ).start()

    zero = jnp.zeros((TILE, TILE), jnp.float32)

    @pl.loop(0, SLOT_DEV)
    def _(s):
        assembled[s] = zero

    head_copy.wait()
    rows = head[...].astype(jnp.float32)
    diagonal = lax.broadcasted_iota(jnp.int32, (peers, TILE), 0) == lax.broadcasted_iota(
        jnp.int32, (peers, TILE), 1
    )
    lane = lax.broadcasted_iota(jnp.int32, (peers, TILE), 1).astype(jnp.float32)
    total = jnp.zeros((TILE, TILE), jnp.float32)
    for r in range(CAP):
        named = jnp.where(diagonal, rows[:, CAP + r, :], 0.0)
        ids_vec[pl.ds(r, 1), :] = jnp.sum(named, axis=0, keepdims=True).astype(jnp.int32)
        select = (rows[:, 2 * CAP + r, :] == lane).astype(jnp.bfloat16)
        total += lax.dot_general(
            select,
            rows[:, r, :].astype(jnp.bfloat16),
            (((0,), (0,)), ((), ())),
            preferred_element_type=jnp.float32,
        )
    ids_copy = pltpu.make_async_copy(ids_vec, ids, ids_sem)
    ids_copy.start()
    loads[...] = total[:VSLOT_DEV]
    ids_copy.wait()

    for c in range(chunks):
        pltpu.make_async_copy(
            got.at[pl.ds(c * width, width), pl.ds(HEAD, CAP * TILE), :], parts.at[c], part_sem.at[c]
        ).wait()

        @pl.loop(0, width)
        def _(w):
            for r in range(CAP):
                s = ids[r, c * width + w]

                @pl.when(s >= 0)
                def _():
                    assembled[s] += parts[c, w, pl.ds(r * TILE, TILE), :].astype(jnp.float32)


def summed(got):
    peers = got.shape[0]
    chunks = 8
    hbm = pl.BlockSpec(memory_space=pltpu.HBM)
    vmem = pl.BlockSpec(memory_space=pltpu.VMEM)
    return pl.pallas_call(
        sum_kernel,
        out_shape=(
            jax.ShapeDtypeStruct((SLOT_DEV, TILE, TILE), jnp.float32),
            jax.ShapeDtypeStruct((VSLOT_DEV, TILE), jnp.float32),
        ),
        in_specs=[hbm],
        out_specs=(vmem, vmem),
        scratch_shapes=[
            pltpu.VMEM((peers, HEAD, TILE), jnp.bfloat16),
            pltpu.VMEM((chunks, peers // chunks, CAP * TILE, TILE), jnp.bfloat16),
            pltpu.VMEM((8, TILE), jnp.int32),
            pltpu.SMEM((8, TILE), jnp.int32),
            pltpu.SemaphoreType.DMA,
            pltpu.SemaphoreType.DMA((chunks,)),
            pltpu.SemaphoreType.DMA,
        ],
        compiler_params=pltpu.CompilerParams(vmem_limit_bytes=48 * MIB),
        name="sum_tiles",
    )(pltpu.with_memory_space_constraint(got, pltpu.HBM))


def shards(
    inv_factor, coupling, boundary, load_int, load_bnd, counts, tile_owner, tile_slot, vec_owner, vec_slot
):
    peers = lax.axis_size("grp") * lax.axis_size("blk")
    send = packed(
        peers,
        inv_factor,
        coupling,
        boundary,
        load_int,
        load_bnd,
        counts,
        jnp.swapaxes(tile_owner, 1, 2),
        tile_slot,
        jnp.swapaxes(vec_owner, 1, 2),
        vec_slot,
    )
    got = lax.all_to_all(send, AXES, split_axis=0, concat_axis=0, tiled=True)
    return summed(got)


def solution(mesh):
    in_specs = (
        P(AXES, None, None),
        P(AXES, None, None),
        P(AXES, None, None),
        P(AXES, None),
        P(AXES, None),
        P(AXES),
        P(AXES, None, None),
        P(AXES, None),
        P(AXES, None, None),
        P(AXES, None),
    )
    out_specs = (P(AXES, None, None), P(AXES, None))
    return jax.shard_map(shards, mesh=mesh, in_specs=in_specs, out_specs=out_specs, check_vma=False)
```

```python
import functools

import jax
import jax.numpy as jnp
from jax import lax
from jax.experimental import pallas as pl
from jax.experimental.pallas import tpu as pltpu
from jax.sharding import PartitionSpec as P

TILE = 128
SLOT_DEV = 64
VSLOT_DEV = 16
CAP = 2
HEAD = 8
WIDE = 256
AXES = ("grp", "blk")
MIB = 1 << 20


def spread(value):
    return jnp.full((1, TILE), value, jnp.int32).astype(jnp.float32)


def row_of(ref, k):
    rows = ref[...].astype(jnp.float32)
    at = lax.broadcasted_iota(jnp.int32, rows.shape, 0) == k
    return jnp.sum(jnp.where(at, rows, 0.0), axis=0, keepdims=True)


def pack_kernel(
    columns,
    counts,
    owner_hbm,
    slot_hbm,
    vowner_hbm,
    vslot_hbm,
    factor_hbm,
    couple_hbm,
    bound_hbm,
    inner_hbm,
    outer_hbm,
    send,
    owner,
    slot,
    vowner,
    vslot,
    inner,
    outer,
    factor,
    couple,
    bound,
    left,
    head,
    used,
    vused,
    target,
    vtarget,
    table_sem,
    in_sem,
):
    emax, ni, nb = couple.shape
    tiles = nb // TILE
    per = tiles * tiles
    peers = used.shape[0]
    tables = [
        pltpu.make_async_copy(source, held, table_sem.at[i])
        for i, (source, held) in enumerate(
            (
                (owner_hbm, owner),
                (slot_hbm, slot),
                (vowner_hbm, vowner),
                (vslot_hbm, vslot),
                (inner_hbm, inner),
                (outer_hbm, outer),
            )
        )
    ]
    for copy in tables:
        copy.start()
    live = counts[0]

    def place_of(device):
        return lax.rem(device, columns) * (peers // columns) + lax.div(device, columns)

    def loads(k):
        return (
            pltpu.make_async_copy(factor_hbm.at[k], factor.at[k], in_sem.at[0, k]),
            pltpu.make_async_copy(couple_hbm.at[k], couple.at[k], in_sem.at[1, k]),
            pltpu.make_async_copy(bound_hbm.at[k], bound.at[k], in_sem.at[2, k]),
        )

    @pl.loop(0, live)
    def _(k):
        for copy in loads(k):
            copy.start()

    row = lax.broadcasted_iota(jnp.int32, (HEAD, TILE), 0)
    blank = jnp.where((row >= CAP) & (row < 3 * CAP), -1.0, 0.0).astype(jnp.float32)

    @pl.loop(0, peers)
    def _(p):
        used[p] = 0
        vused[p] = 0
        head[pl.ds(pl.multiple_of(p * HEAD, HEAD), HEAD), :] = blank

    for copy in tables:
        copy.wait()

    @pl.loop(0, live)
    def _(k):
        @pl.loop(0, per)
        def _(t):
            p = place_of(owner[k, 0, t])
            r = used[p]
            used[p] = r + 1
            target[k * per + t] = p * CAP + r
            head[pl.ds(p * HEAD + CAP + r, 1), :] = spread(slot[k, t])

        @pl.loop(0, tiles)
        def _(t):
            p = place_of(vowner[k, 0, t])
            r = vused[p]
            vused[p] = r + 1
            vtarget[k * tiles + t] = p * HEAD + r
            head[pl.ds(p * HEAD + 2 * CAP + r, 1), :] = spread(vslot[k, t])

    @pl.loop(0, live)
    def _(k):
        for copy in loads(k):
            copy.wait()
        coupled = lax.dot_general(
            couple[k], factor[k], (((0,), (1,)), ((), ())), preferred_element_type=jnp.float32
        ).astype(jnp.bfloat16)
        inner_rows = jnp.broadcast_to(row_of(inner, k), (16, ni)).astype(jnp.bfloat16)
        pulled = lax.dot_general(
            inner_rows, factor[k], (((1,), (1,)), ((), ())), preferred_element_type=jnp.float32
        ).astype(jnp.bfloat16)
        outer_rows = row_of(outer, k)
        left[pl.ds(0, nb), :] = coupled
        left[pl.ds(nb, 16), :] = pulled
        for n in range(nb // WIDE):
            product = lax.dot_general(
                left[...],
                left[pl.ds(n * WIDE, WIDE), :],
                (((1,), (1,)), ((), ())),
                preferred_element_type=jnp.float32,
            )
            for a in range(tiles):
                rows = pl.ds(a * TILE, TILE)
                schur = bound[k, rows, pl.ds(n * WIDE, WIDE)].astype(jnp.float32) - product[a * TILE : (a + 1) * TILE]
                for b in range(WIDE // TILE):
                    to = target[k * per + a * tiles + n * (WIDE // TILE) + b]
                    peer = lax.shift_right_logical(to, 1)
                    start = pl.multiple_of(HEAD + (to & 1) * TILE, HEAD)
                    send[peer, pl.ds(start, TILE), :] = schur[:, b * TILE : (b + 1) * TILE].astype(jnp.bfloat16)
            condensed = outer_rows[:, n * WIDE : (n + 1) * WIDE] - product[nb : nb + 1]
            for b in range(WIDE // TILE):
                at = vtarget[k * tiles + n * (WIDE // TILE) + b]
                head[pl.ds(at, 1), :] = condensed[:, b * TILE : (b + 1) * TILE]

    send[:, pl.ds(0, HEAD), :] = head[...].reshape(peers, HEAD, TILE).astype(jnp.bfloat16)


def packed(columns, peers, inv_factor, coupling, boundary, load_int, load_bnd, counts, owner, slot, vowner, vslot):
    emax, ni, nb = coupling.shape
    tiles = nb // TILE
    per = tiles * tiles
    hbm = pl.BlockSpec(memory_space=pltpu.HBM)
    operands = (owner, slot, vowner, vslot, inv_factor, coupling, boundary, load_int, load_bnd)
    return pl.pallas_call(
        functools.partial(pack_kernel, columns),
        out_shape=pltpu.VMEM((peers, HEAD + CAP * TILE, TILE), jnp.bfloat16),
        in_specs=[pl.BlockSpec(memory_space=pltpu.SMEM)] + [hbm] * len(operands),
        out_specs=pl.BlockSpec(memory_space=pltpu.VMEM),
        scratch_shapes=[
            pltpu.SMEM((emax, 1, per), jnp.int32),
            pltpu.SMEM((emax, per), jnp.int32),
            pltpu.SMEM((emax, 1, tiles), jnp.int32),
            pltpu.SMEM((emax, tiles), jnp.int32),
            pltpu.VMEM((emax, ni), jnp.bfloat16),
            pltpu.VMEM((emax, nb), jnp.bfloat16),
            pltpu.VMEM((emax, ni, ni), jnp.bfloat16),
            pltpu.VMEM((emax, ni, nb), jnp.bfloat16),
            pltpu.VMEM((emax, nb, nb), jnp.bfloat16),
            pltpu.VMEM((nb + 16, ni), jnp.bfloat16),
            pltpu.VMEM((peers * HEAD, TILE), jnp.float32),
            pltpu.SMEM((peers,), jnp.int32),
            pltpu.SMEM((peers,), jnp.int32),
            pltpu.SMEM((emax * per,), jnp.int32),
            pltpu.SMEM((emax * tiles,), jnp.int32),
            pltpu.SemaphoreType.DMA((6,)),
            pltpu.SemaphoreType.DMA((3, emax)),
        ],
        compiler_params=pltpu.CompilerParams(vmem_limit_bytes=48 * MIB),
        name="condense_pack",
    )(counts, *(pltpu.with_memory_space_constraint(x, pltpu.HBM) for x in operands))


def sum_kernel(got, assembled, loads, total, head, parts, ids_vec, ids, head_sem, part_sem, ids_sem, out_sem):
    peers = head.shape[0]
    chunks, width = parts.shape[:2]

    def part_copy(c):
        return pltpu.make_async_copy(
            got.at[pl.ds(c * width, width), pl.ds(HEAD, CAP * TILE), :], parts.at[c], part_sem.at[c]
        )

    head_copy = pltpu.make_async_copy(got.at[:, pl.ds(0, HEAD), :], head, head_sem)
    head_copy.start()
    zero = jnp.zeros((TILE, TILE), jnp.float32)

    @pl.loop(0, SLOT_DEV)
    def _(s):
        total[s] = zero

    head_copy.wait()
    for c in range(chunks):
        part_copy(c).start()
    rows = head[...].astype(jnp.float32)
    diagonal = lax.broadcasted_iota(jnp.int32, (peers, TILE), 0) == lax.broadcasted_iota(
        jnp.int32, (peers, TILE), 1
    )
    lane = lax.broadcasted_iota(jnp.int32, (peers, TILE), 1).astype(jnp.float32)
    vec = jnp.zeros((TILE, TILE), jnp.float32)
    for r in range(CAP):
        named = jnp.where(diagonal, jnp.where(rows[:, CAP + r, :] < 0, SLOT_DEV * 1.0, rows[:, CAP + r, :]), 0.0)
        ids_vec[pl.ds(r, 1), :] = jnp.sum(named, axis=0, keepdims=True).astype(jnp.int32)
        select = (rows[:, 2 * CAP + r, :] == lane).astype(jnp.bfloat16)
        vec += lax.dot_general(
            select,
            rows[:, r, :].astype(jnp.bfloat16),
            (((0,), (0,)), ((), ())),
            preferred_element_type=jnp.float32,
        )
    ids_copy = pltpu.make_async_copy(ids_vec, ids, ids_sem)
    ids_copy.start()
    loads[...] = vec[:VSLOT_DEV]
    ids_copy.wait()

    for c in range(chunks):
        part_copy(c).wait()

        @pl.loop(0, width)
        def _(w):
            for r in range(CAP):
                s = ids[r, c * width + w]
                total[s] += parts[c, w, pl.ds(r * TILE, TILE), :].astype(jnp.float32)

    out_copy = pltpu.make_async_copy(total.at[pl.ds(0, SLOT_DEV)], assembled, out_sem)
    out_copy.start()
    out_copy.wait()


def summed(got):
    peers = got.shape[0]
    chunks = 8
    hbm = pl.BlockSpec(memory_space=pltpu.HBM)
    vmem = pl.BlockSpec(memory_space=pltpu.VMEM)
    return pl.pallas_call(
        sum_kernel,
        out_shape=(
            jax.ShapeDtypeStruct((SLOT_DEV, TILE, TILE), jnp.float32),
            jax.ShapeDtypeStruct((VSLOT_DEV, TILE), jnp.float32),
        ),
        in_specs=[hbm],
        out_specs=(hbm, vmem),
        scratch_shapes=[
            pltpu.VMEM((SLOT_DEV + 1, TILE, TILE), jnp.float32),
            pltpu.VMEM((peers, HEAD, TILE), jnp.bfloat16),
            pltpu.VMEM((chunks, peers // chunks, CAP * TILE, TILE), jnp.bfloat16),
            pltpu.VMEM((8, TILE), jnp.int32),
            pltpu.SMEM((8, TILE), jnp.int32),
            pltpu.SemaphoreType.DMA,
            pltpu.SemaphoreType.DMA((chunks,)),
            pltpu.SemaphoreType.DMA,
            pltpu.SemaphoreType.DMA,
        ],
        compiler_params=pltpu.CompilerParams(vmem_limit_bytes=48 * MIB),
        name="sum_tiles",
    )(pltpu.with_memory_space_constraint(got, pltpu.HBM))


def shards(
    inv_factor, coupling, boundary, load_int, load_bnd, counts, tile_owner, tile_slot, vec_owner, vec_slot
):
    peers = lax.axis_size("grp") * lax.axis_size("blk")
    send = packed(
        lax.axis_size("blk"),
        peers,
        inv_factor,
        coupling,
        boundary,
        load_int,
        load_bnd,
        counts,
        jnp.swapaxes(tile_owner, 1, 2),
        tile_slot,
        jnp.swapaxes(vec_owner, 1, 2),
        vec_slot,
    )
    got = lax.all_to_all(send, ("blk", "grp"), split_axis=0, concat_axis=0, tiled=True)
    return summed(got)


def solution(mesh):
    in_specs = (
        P(AXES, None, None),
        P(AXES, None, None),
        P(AXES, None, None),
        P(AXES, None),
        P(AXES, None),
        P(AXES),
        P(AXES, None, None),
        P(AXES, None),
        P(AXES, None, None),
        P(AXES, None),
    )
    out_specs = (P(AXES, None, None), P(AXES, None))
    return jax.shard_map(shards, mesh=mesh, in_specs=in_specs, out_specs=out_specs, check_vma=False)
```

```python
import functools

import jax
import jax.numpy as jnp
from jax import lax
from jax.experimental import pallas as pl
from jax.experimental.pallas import tpu as pltpu
from jax.sharding import PartitionSpec as P

TILE = 128
SLOT_DEV = 64
VSLOT_DEV = 16
CAP = 2
HEAD = 8
WIDE = 256
AXES = ("grp", "blk")
MIB = 1 << 20


def spread(value):
    return jnp.full((1, TILE), value, jnp.int32).astype(jnp.float32)


def row_of(ref, k):
    rows = ref[...].astype(jnp.float32)
    at = lax.broadcasted_iota(jnp.int32, rows.shape, 0) == k
    return jnp.sum(jnp.where(at, rows, 0.0), axis=0, keepdims=True)


def pack_kernel(
    columns,
    counts,
    owner_hbm,
    slot_hbm,
    vowner_hbm,
    vslot_hbm,
    factor_hbm,
    couple_hbm,
    bound_hbm,
    inner_hbm,
    outer_hbm,
    send,
    owner,
    slot,
    vowner,
    vslot,
    inner,
    outer,
    factor,
    couple,
    bound,
    left,
    head,
    used,
    vused,
    table_sem,
    in_sem,
):
    emax, ni, nb = couple.shape
    tiles = nb // TILE
    per = tiles * tiles
    peers = used.shape[0]
    tables = [
        pltpu.make_async_copy(source, held, table_sem.at[i])
        for i, (source, held) in enumerate(
            (
                (owner_hbm, owner),
                (slot_hbm, slot),
                (vowner_hbm, vowner),
                (vslot_hbm, vslot),
                (inner_hbm, inner),
                (outer_hbm, outer),
            )
        )
    ]
    for copy in tables:
        copy.start()
    live = counts[0]

    def place_of(device):
        shift = columns.bit_length() - 1
        return (device & (columns - 1)) * (peers // columns) + lax.shift_right_logical(device, shift)

    def loads(k):
        return (
            pltpu.make_async_copy(factor_hbm.at[k], factor.at[k], in_sem.at[0, k]),
            pltpu.make_async_copy(couple_hbm.at[k], couple.at[k], in_sem.at[1, k]),
            pltpu.make_async_copy(bound_hbm.at[k], bound.at[k], in_sem.at[2, k]),
        )

    @pl.loop(0, live)
    def _(k):
        for copy in loads(k):
            copy.start()

    row = lax.broadcasted_iota(jnp.int32, (HEAD, TILE), 0)
    blank = jnp.where((row >= CAP) & (row < 3 * CAP), -1.0, 0.0).astype(jnp.float32)

    @pl.loop(0, peers)
    def _(p):
        used[p] = 0
        vused[p] = 0
        head[pl.ds(pl.multiple_of(p * HEAD, HEAD), HEAD), :] = blank

    for copy in tables:
        copy.wait()

    @pl.loop(0, live)
    def _(k):
        for copy in loads(k):
            copy.wait()
        coupled = lax.dot_general(
            couple[k], factor[k], (((0,), (1,)), ((), ())), preferred_element_type=jnp.float32
        ).astype(jnp.bfloat16)
        inner_rows = jnp.broadcast_to(row_of(inner, k), (16, ni)).astype(jnp.bfloat16)
        pulled = lax.dot_general(
            inner_rows, factor[k], (((1,), (1,)), ((), ())), preferred_element_type=jnp.float32
        ).astype(jnp.bfloat16)
        outer_rows = row_of(outer, k)
        left[pl.ds(0, nb), :] = coupled
        left[pl.ds(nb, 16), :] = pulled
        for n in range(nb // WIDE):
            product = lax.dot_general(
                left[...],
                left[pl.ds(n * WIDE, WIDE), :],
                (((1,), (1,)), ((), ())),
                preferred_element_type=jnp.float32,
            )
            for a in range(tiles):
                rows = pl.ds(a * TILE, TILE)
                schur = bound[k, rows, pl.ds(n * WIDE, WIDE)].astype(jnp.float32) - product[a * TILE : (a + 1) * TILE]
                for b in range(WIDE // TILE):
                    t = a * tiles + n * (WIDE // TILE) + b
                    p = place_of(owner[k, 0, t])
                    r = used[p]
                    used[p] = r + 1
                    head[pl.ds(p * HEAD + CAP + r, 1), :] = spread(slot[k, t])
                    start = pl.multiple_of(HEAD + r * TILE, HEAD)
                    send[p, pl.ds(start, TILE), :] = schur[:, b * TILE : (b + 1) * TILE].astype(jnp.bfloat16)
            condensed = outer_rows[:, n * WIDE : (n + 1) * WIDE] - product[nb : nb + 1]
            for b in range(WIDE // TILE):
                t = n * (WIDE // TILE) + b
                p = place_of(vowner[k, 0, t])
                r = vused[p]
                vused[p] = r + 1
                head[pl.ds(p * HEAD + r, 1), :] = condensed[:, b * TILE : (b + 1) * TILE]
                head[pl.ds(p * HEAD + 2 * CAP + r, 1), :] = spread(vslot[k, t])

    send[:, pl.ds(0, HEAD), :] = head[...].reshape(peers, HEAD, TILE).astype(jnp.bfloat16)


def packed(columns, peers, inv_factor, coupling, boundary, load_int, load_bnd, counts, owner, slot, vowner, vslot):
    emax, ni, nb = coupling.shape
    tiles = nb // TILE
    per = tiles * tiles
    hbm = pl.BlockSpec(memory_space=pltpu.HBM)
    operands = (owner, slot, vowner, vslot, inv_factor, coupling, boundary, load_int, load_bnd)
    return pl.pallas_call(
        functools.partial(pack_kernel, columns),
        out_shape=pltpu.VMEM((peers, HEAD + CAP * TILE, TILE), jnp.bfloat16),
        in_specs=[pl.BlockSpec(memory_space=pltpu.SMEM)] + [hbm] * len(operands),
        out_specs=pl.BlockSpec(memory_space=pltpu.VMEM),
        scratch_shapes=[
            pltpu.SMEM((emax, 1, per), jnp.int32),
            pltpu.SMEM((emax, per), jnp.int32),
            pltpu.SMEM((emax, 1, tiles), jnp.int32),
            pltpu.SMEM((emax, tiles), jnp.int32),
            pltpu.VMEM((emax, ni), jnp.bfloat16),
            pltpu.VMEM((emax, nb), jnp.bfloat16),
            pltpu.VMEM((emax, ni, ni), jnp.bfloat16),
            pltpu.VMEM((emax, ni, nb), jnp.bfloat16),
            pltpu.VMEM((emax, nb, nb), jnp.bfloat16),
            pltpu.VMEM((nb + 16, ni), jnp.bfloat16),
            pltpu.VMEM((peers * HEAD, TILE), jnp.float32),
            pltpu.SMEM((peers,), jnp.int32),
            pltpu.SMEM((peers,), jnp.int32),
            pltpu.SemaphoreType.DMA((6,)),
            pltpu.SemaphoreType.DMA((3, emax)),
        ],
        compiler_params=pltpu.CompilerParams(vmem_limit_bytes=48 * MIB),
        name="condense_pack",
    )(counts, *(pltpu.with_memory_space_constraint(x, pltpu.HBM) for x in operands))


def sum_kernel(got, assembled, loads, total, head, parts, ids_vec, ids, head_sem, part_sem, ids_sem, out_sem):
    peers = head.shape[0]
    chunks, width = parts.shape[:2]

    def part_copy(c):
        return pltpu.make_async_copy(
            got.at[pl.ds(c * width, width), pl.ds(HEAD, CAP * TILE), :], parts.at[c], part_sem.at[c]
        )

    head_copy = pltpu.make_async_copy(got.at[:, pl.ds(0, HEAD), :], head, head_sem)
    head_copy.start()
    zero = jnp.zeros((TILE, TILE), jnp.float32)

    @pl.loop(0, SLOT_DEV)
    def _(s):
        total[s] = zero

    head_copy.wait()
    for c in range(chunks):
        part_copy(c).start()
    rows = head[...].astype(jnp.float32)
    diagonal = lax.broadcasted_iota(jnp.int32, (peers, TILE), 0) == lax.broadcasted_iota(
        jnp.int32, (peers, TILE), 1
    )
    lane = lax.broadcasted_iota(jnp.int32, (peers, TILE), 1).astype(jnp.float32)
    vec = jnp.zeros((TILE, TILE), jnp.float32)
    for r in range(CAP):
        named = jnp.where(diagonal, jnp.where(rows[:, CAP + r, :] < 0, SLOT_DEV * 1.0, rows[:, CAP + r, :]), 0.0)
        ids_vec[pl.ds(r, 1), :] = jnp.sum(named, axis=0, keepdims=True).astype(jnp.int32)
        select = (rows[:, 2 * CAP + r, :] == lane).astype(jnp.bfloat16)
        vec += lax.dot_general(
            select,
            rows[:, r, :].astype(jnp.bfloat16),
            (((0,), (0,)), ((), ())),
            preferred_element_type=jnp.float32,
        )
    ids_copy = pltpu.make_async_copy(ids_vec, ids, ids_sem)
    ids_copy.start()
    loads[...] = vec[:VSLOT_DEV]
    ids_copy.wait()

    for c in range(chunks):
        part_copy(c).wait()

        @pl.loop(0, width)
        def _(w):
            for r in range(CAP):
                s = ids[r, c * width + w]
                total[s] += parts[c, w, pl.ds(r * TILE, TILE), :].astype(jnp.float32)

    out_copy = pltpu.make_async_copy(total.at[pl.ds(0, SLOT_DEV)], assembled, out_sem)
    out_copy.start()
    out_copy.wait()


def summed(got):
    peers = got.shape[0]
    chunks = 8
    hbm = pl.BlockSpec(memory_space=pltpu.HBM)
    vmem = pl.BlockSpec(memory_space=pltpu.VMEM)
    return pl.pallas_call(
        sum_kernel,
        out_shape=(
            jax.ShapeDtypeStruct((SLOT_DEV, TILE, TILE), jnp.float32),
            jax.ShapeDtypeStruct((VSLOT_DEV, TILE), jnp.float32),
        ),
        in_specs=[hbm],
        out_specs=(hbm, vmem),
        scratch_shapes=[
            pltpu.VMEM((SLOT_DEV + 1, TILE, TILE), jnp.float32),
            pltpu.VMEM((peers, HEAD, TILE), jnp.bfloat16),
            pltpu.VMEM((chunks, peers // chunks, CAP * TILE, TILE), jnp.bfloat16),
            pltpu.VMEM((8, TILE), jnp.int32),
            pltpu.SMEM((8, TILE), jnp.int32),
            pltpu.SemaphoreType.DMA,
            pltpu.SemaphoreType.DMA((chunks,)),
            pltpu.SemaphoreType.DMA,
            pltpu.SemaphoreType.DMA,
        ],
        compiler_params=pltpu.CompilerParams(vmem_limit_bytes=48 * MIB),
        name="sum_tiles",
    )(pltpu.with_memory_space_constraint(got, pltpu.HBM))


def shards(
    inv_factor, coupling, boundary, load_int, load_bnd, counts, tile_owner, tile_slot, vec_owner, vec_slot
):
    peers = lax.axis_size("grp") * lax.axis_size("blk")
    send = packed(
        lax.axis_size("blk"),
        peers,
        inv_factor,
        coupling,
        boundary,
        load_int,
        load_bnd,
        counts,
        jnp.swapaxes(tile_owner, 1, 2),
        tile_slot,
        jnp.swapaxes(vec_owner, 1, 2),
        vec_slot,
    )
    got = lax.all_to_all(send, ("blk", "grp"), split_axis=0, concat_axis=0, tiled=True)
    return summed(got)


def solution(mesh):
    in_specs = (
        P(AXES, None, None),
        P(AXES, None, None),
        P(AXES, None, None),
        P(AXES, None),
        P(AXES, None),
        P(AXES),
        P(AXES, None, None),
        P(AXES, None),
        P(AXES, None, None),
        P(AXES, None),
    )
    out_specs = (P(AXES, None, None), P(AXES, None))
    return jax.shard_map(shards, mesh=mesh, in_specs=in_specs, out_specs=out_specs, check_vma=False)
```

```python
import functools

import jax
import jax.numpy as jnp
from jax import lax
from jax.experimental import pallas as pl
from jax.experimental.pallas import tpu as pltpu
from jax.sharding import PartitionSpec as P

TILE = 128
SLOT_DEV = 64
VSLOT_DEV = 16
CAP = 2
EXTRA = 16
HEAD = 8
WIDE = 256
AXES = ("grp", "blk")
MIB = 1 << 20


def spread(value):
    return jnp.full((1, TILE), value, jnp.int32).astype(jnp.float32)


def row_of(ref, k):
    rows = ref[...].astype(jnp.float32)
    at = lax.broadcasted_iota(jnp.int32, rows.shape, 0) == k
    return jnp.sum(jnp.where(at, rows, 0.0), axis=0, keepdims=True)


def pack_kernel(
    columns,
    counts,
    owner_hbm,
    slot_hbm,
    vowner_hbm,
    vslot_hbm,
    factor_hbm,
    couple_hbm,
    bound_hbm,
    inner_hbm,
    outer_hbm,
    send,
    owner,
    slot,
    vowner,
    vslot,
    inner,
    outer,
    factor,
    couple,
    bound,
    left,
    head,
    used,
    vused,
    table_sem,
    in_sem,
):
    emax, ni, nb = couple.shape
    tiles = nb // TILE
    per = tiles * tiles
    peers = used.shape[0]
    tables = [
        pltpu.make_async_copy(source, held, table_sem.at[i])
        for i, (source, held) in enumerate(
            (
                (owner_hbm, owner),
                (slot_hbm, slot),
                (vowner_hbm, vowner),
                (vslot_hbm, vslot),
                (inner_hbm, inner),
                (outer_hbm, outer),
            )
        )
    ]
    for copy in tables:
        copy.start()
    live = counts[0]

    def place_of(device):
        shift = columns.bit_length() - 1
        return (device & (columns - 1)) * (peers // columns) + lax.shift_right_logical(device, shift)

    def loads(k):
        return (
            pltpu.make_async_copy(factor_hbm.at[k], factor.at[k], in_sem.at[0, k]),
            pltpu.make_async_copy(couple_hbm.at[k], couple.at[k], in_sem.at[1, k]),
            pltpu.make_async_copy(bound_hbm.at[k], bound.at[k], in_sem.at[2, k]),
        )

    @pl.loop(0, live)
    def _(k):
        for copy in loads(k):
            copy.start()

    row = lax.broadcasted_iota(jnp.int32, (HEAD, TILE), 0)
    blank = jnp.where((row >= CAP) & (row < 3 * CAP), -1.0, 0.0).astype(jnp.float32)

    @pl.loop(0, peers)
    def _(p):
        used[p] = 0
        vused[p] = 0
        head[pl.ds(pl.multiple_of(p * HEAD, HEAD), HEAD), :] = blank

    for copy in tables:
        copy.wait()

    @pl.loop(0, live)
    def _(k):
        for copy in loads(k):
            copy.wait()
        coupled = lax.dot_general(
            couple[k], factor[k], (((0,), (1,)), ((), ())), preferred_element_type=jnp.float32
        ).astype(jnp.bfloat16)
        inner_rows = jnp.broadcast_to(row_of(inner, k), (16, ni)).astype(jnp.bfloat16)
        pulled = lax.dot_general(
            inner_rows, factor[k], (((1,), (1,)), ((), ())), preferred_element_type=jnp.float32
        ).astype(jnp.bfloat16)
        outer_rows = row_of(outer, k)
        left[pl.ds(0, nb), :] = coupled
        left[pl.ds(nb, 16), :] = pulled
        def put(a, b, product):
            t = a * tiles + b
            schur = bound[k, pl.ds(a * TILE, TILE), pl.ds(b * TILE, TILE)].astype(jnp.float32) - product
            p = place_of(owner[k, 0, t])
            r = used[p]
            used[p] = r + 1
            head[pl.ds(p * HEAD + CAP + r, 1), :] = spread(slot[k, t])
            start = pl.multiple_of(HEAD + r * TILE, HEAD)
            send[p, pl.ds(start, TILE), :] = schur.astype(jnp.bfloat16)

        wide = WIDE // TILE
        for n in range(nb // WIDE):
            above = n * WIDE
            product = lax.dot_general(
                left[pl.ds(above, nb + EXTRA - above), :],
                left[pl.ds(above, WIDE), :],
                (((1,), (1,)), ((), ())),
                preferred_element_type=jnp.float32,
            )
            for a in range(n * wide, tiles):
                for b in range(wide):
                    block = product[a * TILE - above : (a + 1) * TILE - above, b * TILE : (b + 1) * TILE]
                    put(a, n * wide + b, block)
                    if a >= (n + 1) * wide:
                        put(n * wide + b, a, block.T)
            condensed = outer_rows[:, n * WIDE : (n + 1) * WIDE] - product[nb - above : nb + 1 - above]
            for b in range(WIDE // TILE):
                t = n * (WIDE // TILE) + b
                p = place_of(vowner[k, 0, t])
                r = vused[p]
                vused[p] = r + 1
                head[pl.ds(p * HEAD + r, 1), :] = condensed[:, b * TILE : (b + 1) * TILE]
                head[pl.ds(p * HEAD + 2 * CAP + r, 1), :] = spread(vslot[k, t])

    send[:, pl.ds(0, HEAD), :] = head[...].reshape(peers, HEAD, TILE).astype(jnp.bfloat16)


def packed(columns, peers, inv_factor, coupling, boundary, load_int, load_bnd, counts, owner, slot, vowner, vslot):
    emax, ni, nb = coupling.shape
    tiles = nb // TILE
    per = tiles * tiles
    hbm = pl.BlockSpec(memory_space=pltpu.HBM)
    operands = (owner, slot, vowner, vslot, inv_factor, coupling, boundary, load_int, load_bnd)
    return pl.pallas_call(
        functools.partial(pack_kernel, columns),
        out_shape=pltpu.VMEM((peers, HEAD + CAP * TILE, TILE), jnp.bfloat16),
        in_specs=[pl.BlockSpec(memory_space=pltpu.SMEM)] + [hbm] * len(operands),
        out_specs=pl.BlockSpec(memory_space=pltpu.VMEM),
        scratch_shapes=[
            pltpu.SMEM((emax, 1, per), jnp.int32),
            pltpu.SMEM((emax, per), jnp.int32),
            pltpu.SMEM((emax, 1, tiles), jnp.int32),
            pltpu.SMEM((emax, tiles), jnp.int32),
            pltpu.VMEM((emax, ni), jnp.bfloat16),
            pltpu.VMEM((emax, nb), jnp.bfloat16),
            pltpu.VMEM((emax, ni, ni), jnp.bfloat16),
            pltpu.VMEM((emax, ni, nb), jnp.bfloat16),
            pltpu.VMEM((emax, nb, nb), jnp.bfloat16),
            pltpu.VMEM((nb + 16, ni), jnp.bfloat16),
            pltpu.VMEM((peers * HEAD, TILE), jnp.float32),
            pltpu.SMEM((peers,), jnp.int32),
            pltpu.SMEM((peers,), jnp.int32),
            pltpu.SemaphoreType.DMA((6,)),
            pltpu.SemaphoreType.DMA((3, emax)),
        ],
        compiler_params=pltpu.CompilerParams(vmem_limit_bytes=48 * MIB),
        name="condense_pack",
    )(counts, *(pltpu.with_memory_space_constraint(x, pltpu.HBM) for x in operands))


def sum_kernel(got, assembled, loads, total, head, parts, ids_vec, ids, head_sem, part_sem, ids_sem, out_sem):
    peers = head.shape[0]
    chunks, width = parts.shape[:2]

    def part_copy(c):
        return pltpu.make_async_copy(
            got.at[pl.ds(c * width, width), pl.ds(HEAD, CAP * TILE), :], parts.at[c], part_sem.at[c]
        )

    head_copy = pltpu.make_async_copy(got.at[:, pl.ds(0, HEAD), :], head, head_sem)
    head_copy.start()
    zero = jnp.zeros((TILE, TILE), jnp.float32)

    @pl.loop(0, SLOT_DEV)
    def _(s):
        total[s] = zero

    head_copy.wait()
    for c in range(chunks):
        part_copy(c).start()
    rows = head[...].astype(jnp.float32)
    diagonal = lax.broadcasted_iota(jnp.int32, (peers, TILE), 0) == lax.broadcasted_iota(
        jnp.int32, (peers, TILE), 1
    )
    lane = lax.broadcasted_iota(jnp.int32, (peers, TILE), 1).astype(jnp.float32)
    vec = jnp.zeros((TILE, TILE), jnp.float32)
    for r in range(CAP):
        named = jnp.where(diagonal, jnp.where(rows[:, CAP + r, :] < 0, SLOT_DEV * 1.0, rows[:, CAP + r, :]), 0.0)
        ids_vec[pl.ds(r, 1), :] = jnp.sum(named, axis=0, keepdims=True).astype(jnp.int32)
        select = (rows[:, 2 * CAP + r, :] == lane).astype(jnp.bfloat16)
        vec += lax.dot_general(
            select,
            rows[:, r, :].astype(jnp.bfloat16),
            (((0,), (0,)), ((), ())),
            preferred_element_type=jnp.float32,
        )
    ids_copy = pltpu.make_async_copy(ids_vec, ids, ids_sem)
    ids_copy.start()
    loads[...] = vec[:VSLOT_DEV]
    ids_copy.wait()

    for c in range(chunks):
        part_copy(c).wait()

        @pl.loop(0, width)
        def _(w):
            for r in range(CAP):
                s = ids[r, c * width + w]
                total[s] += parts[c, w, pl.ds(r * TILE, TILE), :].astype(jnp.float32)

    out_copy = pltpu.make_async_copy(total.at[pl.ds(0, SLOT_DEV)], assembled, out_sem)
    out_copy.start()
    out_copy.wait()


def summed(got):
    peers = got.shape[0]
    chunks = 8
    hbm = pl.BlockSpec(memory_space=pltpu.HBM)
    vmem = pl.BlockSpec(memory_space=pltpu.VMEM)
    return pl.pallas_call(
        sum_kernel,
        out_shape=(
            jax.ShapeDtypeStruct((SLOT_DEV, TILE, TILE), jnp.float32),
            jax.ShapeDtypeStruct((VSLOT_DEV, TILE), jnp.float32),
        ),
        in_specs=[hbm],
        out_specs=(hbm, vmem),
        scratch_shapes=[
            pltpu.VMEM((SLOT_DEV + 1, TILE, TILE), jnp.float32),
            pltpu.VMEM((peers, HEAD, TILE), jnp.bfloat16),
            pltpu.VMEM((chunks, peers // chunks, CAP * TILE, TILE), jnp.bfloat16),
            pltpu.VMEM((8, TILE), jnp.int32),
            pltpu.SMEM((8, TILE), jnp.int32),
            pltpu.SemaphoreType.DMA,
            pltpu.SemaphoreType.DMA((chunks,)),
            pltpu.SemaphoreType.DMA,
            pltpu.SemaphoreType.DMA,
        ],
        compiler_params=pltpu.CompilerParams(vmem_limit_bytes=48 * MIB),
        name="sum_tiles",
    )(pltpu.with_memory_space_constraint(got, pltpu.HBM))


def shards(
    inv_factor, coupling, boundary, load_int, load_bnd, counts, tile_owner, tile_slot, vec_owner, vec_slot
):
    peers = lax.axis_size("grp") * lax.axis_size("blk")
    send = packed(
        lax.axis_size("blk"),
        peers,
        inv_factor,
        coupling,
        boundary,
        load_int,
        load_bnd,
        counts,
        jnp.swapaxes(tile_owner, 1, 2),
        tile_slot,
        jnp.swapaxes(vec_owner, 1, 2),
        vec_slot,
    )
    got = lax.all_to_all(send, ("blk", "grp"), split_axis=0, concat_axis=0, tiled=True)
    return summed(got)


def solution(mesh):
    in_specs = (
        P(AXES, None, None),
        P(AXES, None, None),
        P(AXES, None, None),
        P(AXES, None),
        P(AXES, None),
        P(AXES),
        P(AXES, None, None),
        P(AXES, None),
        P(AXES, None, None),
        P(AXES, None),
    )
    out_specs = (P(AXES, None, None), P(AXES, None))
    return jax.shard_map(shards, mesh=mesh, in_specs=in_specs, out_specs=out_specs, check_vma=False)
```

```python
import functools

import jax
import jax.numpy as jnp
from jax import lax
from jax.experimental import pallas as pl
from jax.experimental.pallas import tpu as pltpu
from jax.sharding import PartitionSpec as P

TILE = 128
SLOT_DEV = 64
VSLOT_DEV = 16
CAP = 2
EXTRA = 16
HEAD = 8
WIDE = 256
AXES = ("grp", "blk")
MIB = 1 << 20


def spread(value):
    return jnp.full((1, TILE), value, jnp.int32).astype(jnp.float32)


def row_of(ref, k):
    rows = ref[...].astype(jnp.float32)
    at = lax.broadcasted_iota(jnp.int32, rows.shape, 0) == k
    return jnp.sum(jnp.where(at, rows, 0.0), axis=0, keepdims=True)


def pack_kernel(
    columns,
    counts,
    owner_hbm,
    slot_hbm,
    vowner_hbm,
    vslot_hbm,
    factor_hbm,
    couple_hbm,
    bound_hbm,
    inner_hbm,
    outer_hbm,
    send,
    owner,
    slot,
    vowner,
    vslot,
    inner,
    outer,
    factor,
    couple,
    bound,
    left,
    head,
    used,
    vused,
    table_sem,
    in_sem,
):
    emax, ni, nb = couple.shape
    tiles = nb // TILE
    per = tiles * tiles
    peers = used.shape[0]
    tables = [
        pltpu.make_async_copy(source, held, table_sem.at[i])
        for i, (source, held) in enumerate(
            (
                (owner_hbm, owner),
                (slot_hbm, slot),
                (vowner_hbm, vowner),
                (vslot_hbm, vslot),
                (inner_hbm, inner),
                (outer_hbm, outer),
            )
        )
    ]
    for copy in tables:
        copy.start()
    live = counts[0]

    def place_of(device):
        shift = columns.bit_length() - 1
        return (device & (columns - 1)) * (peers // columns) + lax.shift_right_logical(device, shift)

    def loads(k):
        return (
            pltpu.make_async_copy(factor_hbm.at[k], factor.at[k], in_sem.at[0, k]),
            pltpu.make_async_copy(couple_hbm.at[k], couple.at[k], in_sem.at[1, k]),
            pltpu.make_async_copy(bound_hbm.at[k], bound.at[k], in_sem.at[2, k]),
        )

    @pl.loop(0, live)
    def _(k):
        for copy in loads(k):
            copy.start()

    row = lax.broadcasted_iota(jnp.int32, (HEAD, TILE), 0)
    blank = jnp.where((row >= CAP) & (row < 3 * CAP), -1.0, 0.0).astype(jnp.float32)

    @pl.loop(0, peers)
    def _(p):
        used[p] = 0
        vused[p] = 0
        head[pl.ds(pl.multiple_of(p * HEAD, HEAD), HEAD), :] = blank

    for copy in tables:
        copy.wait()

    @pl.loop(0, live)
    def _(k):
        for copy in loads(k):
            copy.wait()
        coupled = lax.dot_general(
            couple[k], factor[k], (((0,), (1,)), ((), ())), preferred_element_type=jnp.float32
        ).astype(jnp.bfloat16)
        inner_rows = jnp.broadcast_to(row_of(inner, k), (16, ni)).astype(jnp.bfloat16)
        pulled = lax.dot_general(
            inner_rows, factor[k], (((1,), (1,)), ((), ())), preferred_element_type=jnp.float32
        ).astype(jnp.bfloat16)
        outer_rows = row_of(outer, k)
        left[pl.ds(0, nb), :] = coupled
        left[pl.ds(nb, 16), :] = pulled
        def put(a, b, product):
            t = a * tiles + b
            schur = bound[k, pl.ds(a * TILE, TILE), pl.ds(b * TILE, TILE)].astype(jnp.float32) - product
            p = place_of(owner[k, 0, t])
            r = used[p]
            used[p] = r + 1
            head[pl.ds(p * HEAD + CAP + r, 1), :] = spread(slot[k, t])
            start = pl.multiple_of(HEAD + r * TILE, HEAD)
            send[p, pl.ds(start, TILE), :] = schur.astype(jnp.bfloat16)

        wide = WIDE // TILE
        for n in range(nb // WIDE):
            above = n * WIDE
            product = lax.dot_general(
                left[pl.ds(above, nb + EXTRA - above), :],
                left[pl.ds(above, WIDE), :],
                (((1,), (1,)), ((), ())),
                preferred_element_type=jnp.float32,
            )
            for a in range(n * wide, tiles):
                for b in range(wide):
                    block = product[a * TILE - above : (a + 1) * TILE - above, b * TILE : (b + 1) * TILE]
                    put(a, n * wide + b, block)
                    if a >= (n + 1) * wide:
                        put(n * wide + b, a, block.T)
            condensed = outer_rows[:, n * WIDE : (n + 1) * WIDE] - product[nb - above : nb + 1 - above]
            for b in range(WIDE // TILE):
                t = n * (WIDE // TILE) + b
                p = place_of(vowner[k, 0, t])
                r = vused[p]
                vused[p] = r + 1
                head[pl.ds(p * HEAD + r, 1), :] = condensed[:, b * TILE : (b + 1) * TILE]
                head[pl.ds(p * HEAD + 2 * CAP + r, 1), :] = spread(vslot[k, t])

    send[:, pl.ds(0, HEAD), :] = head[...].reshape(peers, HEAD, TILE).astype(jnp.bfloat16)


def packed(columns, peers, inv_factor, coupling, boundary, load_int, load_bnd, counts, owner, slot, vowner, vslot):
    emax, ni, nb = coupling.shape
    tiles = nb // TILE
    per = tiles * tiles
    hbm = pl.BlockSpec(memory_space=pltpu.HBM)
    operands = (owner, slot, vowner, vslot, inv_factor, coupling, boundary, load_int, load_bnd)
    return pl.pallas_call(
        functools.partial(pack_kernel, columns),
        out_shape=pltpu.VMEM((peers, HEAD + CAP * TILE, TILE), jnp.bfloat16),
        in_specs=[pl.BlockSpec(memory_space=pltpu.SMEM)] + [hbm] * len(operands),
        out_specs=pl.BlockSpec(memory_space=pltpu.VMEM),
        scratch_shapes=[
            pltpu.SMEM((emax, 1, per), jnp.int32),
            pltpu.SMEM((emax, per), jnp.int32),
            pltpu.SMEM((emax, 1, tiles), jnp.int32),
            pltpu.SMEM((emax, tiles), jnp.int32),
            pltpu.VMEM((emax, ni), jnp.bfloat16),
            pltpu.VMEM((emax, nb), jnp.bfloat16),
            pltpu.VMEM((emax, ni, ni), jnp.bfloat16),
            pltpu.VMEM((emax, ni, nb), jnp.bfloat16),
            pltpu.VMEM((emax, nb, nb), jnp.bfloat16),
            pltpu.VMEM((nb + 16, ni), jnp.bfloat16),
            pltpu.VMEM((peers * HEAD, TILE), jnp.float32),
            pltpu.SMEM((peers,), jnp.int32),
            pltpu.SMEM((peers,), jnp.int32),
            pltpu.SemaphoreType.DMA((6,)),
            pltpu.SemaphoreType.DMA((3, emax)),
        ],
        compiler_params=pltpu.CompilerParams(vmem_limit_bytes=48 * MIB),
        name="condense_pack",
    )(counts, *(pltpu.with_memory_space_constraint(x, pltpu.HBM) for x in operands))


def sum_kernel(got, assembled, loads, total, head, parts, ids_vec, ids, head_sem, part_sem, ids_sem, out_sem):
    peers = head.shape[0]
    chunks, width = parts.shape[:2]

    def part_copy(c):
        return pltpu.make_async_copy(
            got.at[pl.ds(c * width, width), pl.ds(HEAD, CAP * TILE), :], parts.at[c], part_sem.at[c]
        )

    head_copy = pltpu.make_async_copy(got.at[:, pl.ds(0, HEAD), :], head, head_sem)
    head_copy.start()
    zero = jnp.zeros((TILE, TILE), jnp.float32)

    @pl.loop(0, SLOT_DEV)
    def _(s):
        total[s] = zero

    head_copy.wait()
    for c in range(chunks):
        part_copy(c).start()
    rows = head[...].astype(jnp.float32)
    diagonal = lax.broadcasted_iota(jnp.int32, (peers, TILE), 0) == lax.broadcasted_iota(
        jnp.int32, (peers, TILE), 1
    )
    lane = lax.broadcasted_iota(jnp.int32, (peers, TILE), 1).astype(jnp.float32)
    for r in range(CAP):
        named = jnp.where(rows[:, CAP + r, :] < 0, float(SLOT_DEV), rows[:, CAP + r, :])
        ids_vec[pl.ds(r, 1), :] = jnp.sum(jnp.where(diagonal, named, 0.0), axis=0, keepdims=True).astype(jnp.int32)
    ids_copy = pltpu.make_async_copy(ids_vec, ids, ids_sem)
    ids_copy.start()
    vec = jnp.zeros((TILE, TILE), jnp.float32)
    for r in range(CAP):
        select = (rows[:, 2 * CAP + r, :] == lane).astype(jnp.bfloat16)
        vec += lax.dot_general(
            select,
            rows[:, r, :].astype(jnp.bfloat16),
            (((0,), (0,)), ((), ())),
            preferred_element_type=jnp.float32,
        )
    loads[...] = vec[:VSLOT_DEV]
    ids_copy.wait()

    for c in range(chunks):
        part_copy(c).wait()

        @pl.loop(0, width, unroll=4)
        def _(w):
            for r in range(CAP):
                s = ids[r, c * width + w]
                total[s] += parts[c, w, pl.ds(r * TILE, TILE), :].astype(jnp.float32)

    out_copy = pltpu.make_async_copy(total.at[pl.ds(0, SLOT_DEV)], assembled, out_sem)
    out_copy.start()
    out_copy.wait()


def summed(got):
    peers = got.shape[0]
    chunks = 8
    hbm = pl.BlockSpec(memory_space=pltpu.HBM)
    vmem = pl.BlockSpec(memory_space=pltpu.VMEM)
    return pl.pallas_call(
        sum_kernel,
        out_shape=(
            jax.ShapeDtypeStruct((SLOT_DEV, TILE, TILE), jnp.float32),
            jax.ShapeDtypeStruct((VSLOT_DEV, TILE), jnp.float32),
        ),
        in_specs=[hbm],
        out_specs=(hbm, vmem),
        scratch_shapes=[
            pltpu.VMEM((SLOT_DEV + 1, TILE, TILE), jnp.float32),
            pltpu.VMEM((peers, HEAD, TILE), jnp.bfloat16),
            pltpu.VMEM((chunks, peers // chunks, CAP * TILE, TILE), jnp.bfloat16),
            pltpu.VMEM((8, TILE), jnp.int32),
            pltpu.SMEM((8, TILE), jnp.int32),
            pltpu.SemaphoreType.DMA,
            pltpu.SemaphoreType.DMA((chunks,)),
            pltpu.SemaphoreType.DMA,
            pltpu.SemaphoreType.DMA,
        ],
        compiler_params=pltpu.CompilerParams(vmem_limit_bytes=48 * MIB),
        name="sum_tiles",
    )(pltpu.with_memory_space_constraint(got, pltpu.HBM))


def shards(
    inv_factor, coupling, boundary, load_int, load_bnd, counts, tile_owner, tile_slot, vec_owner, vec_slot
):
    peers = lax.axis_size("grp") * lax.axis_size("blk")
    send = packed(
        lax.axis_size("blk"),
        peers,
        inv_factor,
        coupling,
        boundary,
        load_int,
        load_bnd,
        counts,
        jnp.swapaxes(tile_owner, 1, 2),
        tile_slot,
        jnp.swapaxes(vec_owner, 1, 2),
        vec_slot,
    )
    got = lax.all_to_all(send, ("blk", "grp"), split_axis=0, concat_axis=0, tiled=True)
    return summed(got)


def solution(mesh):
    in_specs = (
        P(AXES, None, None),
        P(AXES, None, None),
        P(AXES, None, None),
        P(AXES, None),
        P(AXES, None),
        P(AXES),
        P(AXES, None, None),
        P(AXES, None),
        P(AXES, None, None),
        P(AXES, None),
    )
    out_specs = (P(AXES, None, None), P(AXES, None))
    return jax.shard_map(shards, mesh=mesh, in_specs=in_specs, out_specs=out_specs, check_vma=False)
```
